32 devices in a mesh: group: 2 (over y), seq: 4 (over z), dp: 2 (over x), head: 2 (over core).
Axes of the slice: x: 2, y: 2, z: 4, core: 2. Of those that a mesh axis runs over, the one named last changes fastest.
Arguments:
- query_raw: bfloat16 [4, 512, 2048], P(('group', 'dp'), 'seq', 'head'), parts along dimension 0, may hold values from -6 to 6
- key_raw: bfloat16 [4, 512, 2048], P(('group', 'dp'), 'seq', 'head'), parts along dimension 0, may hold values from -6 to 6
- value_raw: bfloat16 [4, 512, 2048], P(('group', 'dp'), 'seq', 'head'), parts along dimension 0, may hold values from -12 to 12
- conv_weight: float32 [3, 4, 2048], P(None, None, 'head'), may hold values from -2.4 to 2.4
- beta_logit: float32 [4, 16, 512], P(('group', 'dp'), 'head', 'seq'), parts along dimension 0, may hold values from -14 to 9
- cotangent: bfloat16 [4, 512, 2048], P(('group', 'dp'), 'seq', 'head'), parts along dimension 0, may hold values from -6 to 6
Outputs:
- mixed: float32 [4, 512, 2048], P(('group', 'dp'), 'seq', 'head'), parts along dimension 0
- query_grad: bfloat16 [4, 512, 2048], P(('group', 'dp'), 'seq', 'head'), parts along dimension 0
- key_grad: bfloat16 [4, 512, 2048], P(('group', 'dp'), 'seq', 'head'), parts along dimension 0
- value_grad: bfloat16 [4, 512, 2048], P(('group', 'dp'), 'seq', 'head'), parts along dimension 0
- beta_grad: float32 [4, 16, 512], P(('group', 'dp'), 'head', 'seq'), parts along dimension 0
- conv_grad: float32 [6, 4, 16, 128], P('group', None, 'head', ('seq', 'dp')), parts along dimension 0
The draws below stay inside these ranges and needn't reach their ends.
There are 2 independent parts, one for each index of `group`. The reference program is written for one: setup_inputs(seed, part) draws one part's arguments, and reference() takes and returns one part's arrays. A program takes and returns all parts, laid end to end along the dimension named above; an argument that names none is the same for every part. Nothing has to cross between parts.
All inputs are finite; a program needn't handle non-finite values.
Results may differ from the reference program's by a relative error of at most 0.0023.
Values may be sent and summed in bfloat16 or wider, within the bound.
A program may use at most 128 MiB of HBM per device.

```python
import jax
import jax.numpy as jnp
from jax import lax

DK = 128
HEADS = 16
SPAN = 64
TAPS = 4
TOKEN_COUNT = 512
BATCH = 2


def draw_beta_logit(key, part):
    tensor_dimensions = (BATCH, HEADS, TOKEN_COUNT)
    lookup_vectors = jax.random.split(jax.random.fold_in(key, 7), 5)
    slow_base = jnp.log(DK / (2.0 * TOKEN_COUNT))
    slow_share = 0.5
    random_samples = 0.8 * jax.random.normal(lookup_vectors[2], tensor_dimensions, jnp.float32)
    picker = jax.random.uniform(lookup_vectors[0], (BATCH, HEADS, 1), jnp.float32)
    slow_level = slow_base + jax.random.uniform(lookup_vectors[1], (BATCH, HEADS, 1), jnp.float32, -1.0, 1.0)
    fast_level = jax.random.uniform(lookup_vectors[3], (BATCH, HEADS, 1), jnp.float32, -1.0, 2.0)
    magnitude_factor = jnp.where(picker < slow_share, slow_level, fast_level)
    cluster_bundles = jax.random.uniform(lookup_vectors[4], tensor_dimensions, jnp.float32) < 8.0 / TOKEN_COUNT
    payload_vectors = magnitude_factor + random_samples + jnp.where(cluster_bundles, 7.0, 0.0)
    return jnp.clip(payload_vectors, -14.0, 9.0).astype(jnp.float32)


def level_of(key, extent, cuts, least, top_value):
    gain = 1.0
    for position, parts in cuts:
        heights = jax.random.uniform(jax.random.fold_in(jax.random.fold_in(key, 6), position), (parts,), jnp.float32, least / len(cuts), top_value / len(cuts))
        gain = gain * jnp.repeat(jnp.exp(heights), extent[position] // parts).reshape((-1,) + (1,) * (len(extent) - 1 - position))
    return gain


def normal_values(key, extent, scale, most, cuts=(), kind=jnp.bfloat16):
    values = scale * jax.random.normal(key, extent, jnp.float32)
    if cuts:
        values = values * level_of(key, extent, cuts, -0.22, 0.18)
    return jnp.clip(values, -most, most).astype(kind)


def setup_inputs(seed: int = 0, part: int = 0) -> dict:
    seeds = jax.random.split(jax.random.key(seed), 7)
    part_splits = jax.random.split(jax.random.fold_in(seeds[6], part), 7)
    query_raw = normal_values(part_splits[0], (BATCH, TOKEN_COUNT, HEADS * DK), 1.0, 6.0, ((0, 2), (1, 4), (2, 2)))
    key_raw = normal_values(part_splits[1], (BATCH, TOKEN_COUNT, HEADS * DK), 1.0, 6.0, ((0, 2), (1, 4), (2, 2)))
    value_raw = normal_values(part_splits[2], (BATCH, TOKEN_COUNT, HEADS * DK), 2.0, 12.0, ((0, 2), (1, 4), (2, 2)))
    conv_weight = normal_values(seeds[3], (3, TAPS, HEADS * DK), 0.6, 2.4, ((2, 2),), jnp.float32)
    beta_logit = draw_beta_logit(jax.random.fold_in(jax.random.fold_in(seeds[6], part), 71), part)
    cotangent = normal_values(part_splits[5], (BATCH, TOKEN_COUNT, HEADS * DK), 1.0, 6.0, ((0, 2), (1, 4), (2, 2)))
    return {"query_raw": query_raw, "key_raw": key_raw, "value_raw": value_raw, "conv_weight": conv_weight, "beta_logit": beta_logit, "cotangent": cotangent}


def strict_lower(count):
    return jnp.tril(jnp.ones((count, count), jnp.float32), -1)

def solve_block(lookup_vectors, payload_vectors, betas):
    count = lookup_vectors.shape[-2]
    width = lookup_vectors.shape[-1]
    inner = jnp.einsum('...id,...jd->...ij', lookup_vectors, lookup_vectors, precision=lax.Precision.HIGHEST)
    lower_part = betas[..., :, None] * inner * strict_lower(count)
    eye_block = jnp.eye(count, dtype=jnp.float32)
    inverse = eye_block - lower_part
    power_term = lower_part
    reach = 2
    while reach < count:
        power_term = jnp.einsum('...ij,...jk->...ik', power_term, power_term, precision=lax.Precision.HIGHEST)
        inverse = jnp.einsum('...ij,...jk->...ik', inverse, eye_block + power_term, precision=lax.Precision.HIGHEST)
        reach = reach * 2
    right_side = betas[..., :, None] * jnp.concatenate([lookup_vectors, payload_vectors], axis=-1)
    solved = jnp.einsum('...ij,...jk->...ik', inverse, right_side, precision=lax.Precision.HIGHEST)
    return (solved[..., :width], solved[..., width:])

def block_step(memory, inputs):
    queries, lookup_vectors, payload_vectors, betas = inputs
    w_rows, u_rows = solve_block(lookup_vectors, payload_vectors, betas)
    corrected = u_rows - jnp.einsum('...cd,...de->...ce', w_rows, memory, precision=lax.Precision.HIGHEST)
    count = lookup_vectors.shape[-2]
    causal = jnp.tril(jnp.ones((count, count), jnp.float32))
    scores = jnp.einsum('...id,...jd->...ij', queries, lookup_vectors, precision=lax.Precision.HIGHEST) * causal
    result = jnp.einsum('...cd,...de->...ce', queries, memory, precision=lax.Precision.HIGHEST)
    result = result + jnp.einsum('...ij,...je->...ie', scores, corrected, precision=lax.Precision.HIGHEST)
    memory = memory + jnp.einsum('...cd,...ce->...de', lookup_vectors, corrected, precision=lax.Precision.HIGHEST)
    return (memory, result)

def to_blocks(active, heads):
    batch, length, total = active.shape
    width = total // heads
    return active.reshape(batch, length // SPAN, SPAN, heads, width).transpose(1, 0, 3, 2, 4)

def from_blocks(blocks):
    count, batch, heads, block_len, width = blocks.shape
    return blocks.transpose(1, 0, 3, 2, 4).reshape(batch, count * block_len, heads * width)

def normalize(blocks):
    return blocks * lax.rsqrt(lax.optimization_barrier(jnp.sum(blocks * blocks, axis=-1, keepdims=True)) + 1e-06)

def prepare(query_ext, key_ext, value_ext, taps_all, logits):
    heads = logits.shape[1]
    margin = taps_all.shape[1] - 1
    length = query_ext.shape[1] - margin

    def convolve(series, taps):
        total = taps[0][None, None, :] * series[:, 0:length]
        for offset in range(1, margin + 1):
            total = total + taps[offset][None, None, :] * series[:, offset:offset + length]
        return total
    queries = normalize(to_blocks(jax.nn.silu(convolve(query_ext, taps_all[0])), heads))
    lookup_vectors = normalize(to_blocks(jax.nn.silu(convolve(key_ext, taps_all[1])), heads))
    payload_vectors = to_blocks(jax.nn.silu(convolve(value_ext, taps_all[2])), heads)
    batch = logits.shape[0]
    betas = jax.nn.sigmoid(logits).reshape(batch, heads, length // SPAN, SPAN).transpose(2, 0, 1, 3)
    return (queries, lookup_vectors, payload_vectors, betas)

def reference(query_raw, key_raw, value_raw, conv_weight, beta_logit, cotangent):
    heads = beta_logit.shape[1]
    width = query_raw.shape[2] // heads
    margin = conv_weight.shape[1] - 1

    def sequence(items):
        query_one, key_one, value_one, logit_one, cot_one = items

        def forward(query_in, key_in, value_in, taps_all, logits):
            pad_rows = jnp.zeros((margin, query_in.shape[1]), jnp.float32)
            query_ext = jnp.concatenate([pad_rows, query_in], axis=0)[None]
            key_ext = jnp.concatenate([pad_rows, key_in], axis=0)[None]
            value_ext = jnp.concatenate([pad_rows, value_in], axis=0)[None]
            blocks = prepare(query_ext, key_ext, value_ext, taps_all, logits[None])
            start = jnp.zeros((1, heads, width, width), jnp.float32)
            final, outputs = lax.scan(block_step, start, blocks)
            return from_blocks(outputs)[0]
        mixed_one, pullback = jax.vjp(forward, query_one.astype(jnp.float32), key_one.astype(jnp.float32), value_one.astype(jnp.float32), conv_weight, logit_one)
        grads = pullback(cot_one.astype(jnp.float32))
        return (mixed_one, grads[0].astype(jnp.bfloat16), grads[1].astype(jnp.bfloat16), grads[2].astype(jnp.bfloat16), grads[4], grads[3])
    results = lax.map(sequence, (query_raw, key_raw, value_raw, beta_logit, cotangent))
    conv_grad = lax.optimization_barrier(jnp.sum(results[5], axis=0)).reshape(3, conv_weight.shape[1], heads, width)
    return (results[0], results[1], results[2], results[3], results[4], conv_grad)
```

```python
import functools

import jax
import jax.numpy as jnp
from jax import lax
from jax.experimental import pallas as pl
from jax.experimental.pallas import tpu as pltpu
from jax.sharding import PartitionSpec as P

MESH = pl.DeviceIdType.MESH
F32 = jnp.float32
BF16 = jnp.bfloat16
SKEW = 2
GROUP = 4


def split(x):
    high = x.astype(BF16)
    return high, (x - high.astype(F32)).astype(BF16)


def whole(x):
    return x.astype(BF16), None


def mm(a, b, flip=False):
    ah, al = a
    bh, bl = b
    lhs = ah if al is None else jnp.concatenate([ah, al], axis=1)
    if flip:
        axis_n, axis_k = 0, 1
    else:
        axis_n, axis_k = 1, 0
    n = bh.shape[axis_n]
    rhs = bh if bl is None else jnp.concatenate([bh, bl], axis=axis_n)
    if al is not None:
        rhs = jnp.concatenate([rhs, rhs], axis=axis_k)
    out = lax.dot_general(
        lhs, rhs, (((1,), (axis_k,)), ((), ())), preferred_element_type=F32
    )
    if bl is not None:
        out = out[:, :n] + out[:, n:]
    return out


def kernel(
    shards, parts, scatter,
    q_raw, k_raw, v_raw, conv_ref, beta_ref, cot_ref,
    mixed_ref, dq_ref, dk_ref, dv_ref, dbeta_ref, conv_out,
    halo, q_s, k_s, v_s, g_s, p_s, gram_s, inv_s, wu_s, r_s, n_s, nt_s,
    out_state, out_adj, in_state, in_adj, edge_out, edge_in, tail, cg, cgt, gathered,
    halo_send, halo_recv, state_send, state_recv, adj_send, adj_recv,
    edge_send, edge_recv, cg_send, cg_recv,
):
    z = lax.axis_index("seq")
    heads = beta_ref.shape[0]
    count, width = q_raw.shape[0], q_raw.shape[1] // heads
    first, last = z == 0, z == shards - 1
    raws = (q_raw, k_raw, v_raw)
    grads = (dq_ref, dk_ref, dv_ref)

    barrier = pltpu.get_barrier_semaphore()
    if scatter:
        total = shards * parts
        mine = z * parts + lax.axis_index("dp")

        def peer_of(step):
            peer = lax.rem(mine + step, total)
            return peer, {"seq": peer // parts, "dp": lax.rem(peer, parts)}

        for step in range(1, total):
            pl.semaphore_signal(barrier, inc=1, device_id=peer_of(step)[1], device_id_type=MESH)
        pl.semaphore_wait(barrier, total - 1)
    else:
        @pl.when(z > 0)
        def _():
            pl.semaphore_signal(barrier, inc=1, device_id={"seq": z - 1}, device_id_type=MESH)

        @pl.when(z < shards - 1)
        def _():
            pl.semaphore_signal(barrier, inc=1, device_id={"seq": z + 1}, device_id_type=MESH)

        @pl.when(z > 0)
        def _():
            pl.semaphore_wait(barrier, 1)

        @pl.when(z < shards - 1)
        def _():
            pl.semaphore_wait(barrier, 1)

    def halo_copy(s):
        return pltpu.make_async_remote_copy(
            src_ref=raws[s].at[pl.ds(count - 16, 16), :], dst_ref=halo.at[s],
            send_sem=halo_send.at[s], recv_sem=halo_recv.at[s],
            device_id={"seq": z + 1}, device_id_type=MESH,
        )

    def state_copy(h):
        return pltpu.make_async_remote_copy(
            src_ref=out_state.at[h], dst_ref=in_state.at[h],
            send_sem=state_send.at[h], recv_sem=state_recv.at[h],
            device_id={"seq": z + 1}, device_id_type=MESH,
        )

    def adj_copy(h):
        return pltpu.make_async_remote_copy(
            src_ref=out_adj.at[h], dst_ref=in_adj.at[h],
            send_sem=adj_send.at[h], recv_sem=adj_recv.at[h],
            device_id={"seq": z - 1}, device_id_type=MESH,
        )

    def edge_copy(h):
        return pltpu.make_async_remote_copy(
            src_ref=edge_out.at[h], dst_ref=edge_in.at[h],
            send_sem=edge_send.at[h], recv_sem=edge_recv.at[h],
            device_id={"seq": z - 1}, device_id_type=MESH,
        )

    @pl.when(z < shards - 1)
    def _():
        for s in range(3):
            halo_copy(s).start()

    @pl.when(first)
    def _():
        halo[...] = jnp.zeros_like(halo)
        in_state[...] = jnp.zeros_like(in_state)

    @pl.when(last)
    def _():
        in_adj[...] = jnp.zeros_like(in_adj)
        edge_in[...] = jnp.zeros_like(edge_in)

    cg[...] = jnp.zeros_like(cg)
    rows = lax.broadcasted_iota(jnp.int32, (count, count), 0)
    cols = lax.broadcasted_iota(jnp.int32, (count, count), 1)
    apart = rows ^ cols
    strict = rows > cols
    lower = rows >= cols
    eye = rows == cols

    def beta_of(h):
        row = 1.0 / (1.0 + jnp.exp(-beta_ref[pl.ds(h, 1), :]))
        return row, jnp.sum(jnp.where(eye, row, 0.0), axis=1, keepdims=True)

    def lanes_of(h):
        return pl.ds(pl.multiple_of(h * width, width), width)

    def series_of(s, h):
        before = halo[s, :, lanes_of(h)].astype(F32)[8:]
        return jnp.concatenate([before, raws[s][:, lanes_of(h)].astype(F32)], axis=0)

    @pl.when(z > 0)
    def _():
        for s in range(3):
            halo_copy(s).wait_recv()

    def prepare(step, carry):
        ids = [step * GROUP + i for i in range(GROUP)]
        qs, ks, vs = [], [], []
        for h in ids:
            lanes = lanes_of(h)
            made = []
            for s in range(3):
                ext = series_of(s, h)
                pre = conv_ref[pl.ds(s * 4, 1), lanes] * ext[5:5 + count]
                for j in range(1, 4):
                    pre = pre + conv_ref[pl.ds(s * 4 + j, 1), lanes] * ext[5 + j:5 + j + count]
                gate = 1.0 / (1.0 + jnp.exp(-pre))
                act = pre * gate
                slope = gate * (1.0 + pre * (1.0 - gate))
                if s < 2:
                    scale = lax.rsqrt(jnp.sum(act * act, axis=1, keepdims=True) + 1e-06)
                    act = act * scale
                    slope = slope * scale
                g_s[s, h] = slope
                made.append(act)
            q_s[h], k_s[h], v_s[h] = made
            qs.append(made[0])
            ks.append(made[1])
            vs.append(made[2])
        k2 = [split(k) for k in ks]
        gram = [mm(k, k, True) for k in k2]
        score = [jnp.where(lower, mm(split(q), k, True), 0.0) for q, k in zip(qs, k2)]
        betas = [beta_of(h) for h in ids]
        low = [jnp.where(strict, b[1] * g, 0.0) for b, g in zip(betas, gram)]
        inv = [jnp.where(eye, 1.0, 0.0) - jnp.where(apart < 2, a, 0.0) for a in low]
        size = 2
        while size < count:
            band = (apart >= size) & (apart < 2 * size)
            i2 = [split(m) for m in inv]
            part = [mm(split(jnp.where(band, a, 0.0)), m) for a, m in zip(low, i2)]
            inv = [m - mm(n, split(x)) for m, n, x in zip(inv, i2, part)]
            size *= 2
        wu = [
            mm(split(m * b[0]), split(jnp.concatenate([k, v], axis=1)))
            for m, b, k, v in zip(inv, betas, ks, vs)
        ]
        nb = [mm(split(k.T), split(x)) for k, x in zip(ks, wu)]
        reader = [q - mm(split(p), split(x[:, :width])) for q, p, x in zip(qs, score, wu)]
        source = [
            mm(split(r.T), (cot_ref[:, lanes_of(h)], None)) for r, h in zip(reader, ids)
        ]
        for i, h in enumerate(ids):
            out_state[h] = nb[i][:, width:]
            out_adj[h] = source[i]
            p_s[h] = score[i]
            gram_s[h] = gram[i]
            inv_s[h] = inv[i]
            wu_s[h] = wu[i]
            r_s[h] = reader[i]
            n_s[h] = jnp.concatenate(split(nb[i][:, :width]), axis=1)
            nt_s[h] = jnp.concatenate(split(nb[i][:, :width].T), axis=1)

        @pl.when(first)
        def _():
            for h in ids:
                state_copy(h).start()

        @pl.when(last)
        def _():
            for h in ids:
                adj_copy(h).start()

        return carry

    lax.fori_loop(0, heads // GROUP, prepare, 0)

    def advance(pair, value):
        high, low = split(value)
        both = jnp.concatenate([high, low], axis=1)
        out = jnp.dot(pair, jnp.concatenate([both, both], axis=0), preferred_element_type=F32)
        return value - (out[:, :width] + out[:, width:])

    def finish(h):
        lanes = lanes_of(h)
        cot = cot_ref[:, lanes]
        query, key, value = q_s[h], k_s[h], v_s[h]
        score, wu, reader = p_s[h], wu_s[h], r_s[h]
        w_rows, u_rows = wu[:, :width], wu[:, width:]
        state2, adj2 = split(in_state[h]), split(in_adj[h])
        key2 = split(key)
        beta_row, beta_col = beta_of(h)
        reads = mm(split(jnp.concatenate([w_rows, reader], axis=0)), state2)
        corrected = u_rows - reads[:count]
        mixed_ref[:, lanes] = reads[count:] + mm(split(score), split(u_rows))
        d_corr = mm(split(score.T), (cot, None)) + mm(key2, adj2)
        corr2 = split(corrected)
        d_score = jnp.where(lower, mm((cot, None), corr2, True), 0.0)
        back = mm(split(jnp.concatenate([cot.astype(F32), d_corr], axis=0)), state2, True)
        y = mm(split(inv_s[h].T), split(jnp.concatenate([-back[count:], d_corr], axis=1)))
        y_k, y_v = y[:, :width], y[:, width:]
        d_low = jnp.where(strict, -mm(split(y), split(wu), True), 0.0)
        d_beta = jnp.sum(y_k * key + y_v * value + d_low * gram_s[h], axis=1, keepdims=True)
        d_gram = beta_col * d_low
        onto = mm(split(jnp.concatenate([d_score, d_gram + d_gram.T], axis=0)), key2)
        d_query = back[:count] + onto[:count]
        d_key = (
            mm(split(d_score.T), split(query)) + mm(corr2, adj2, True)
            + beta_col * y_k + onto[count:]
        )
        d_value = beta_col * y_v
        d_row = jnp.sum(jnp.where(eye, d_beta, 0.0), axis=0, keepdims=True)
        dbeta_ref[pl.ds(h, 1), :] = d_row * beta_row * (1.0 - beta_row)
        blank = jnp.zeros((8, width), F32)
        for s, grad in enumerate((d_query, d_key, d_value)):
            if s < 2:
                unit = (query, key)[s]
                grad = grad - unit * jnp.sum(grad * unit, axis=1, keepdims=True)
            d_pre = grad * g_s[s, h]
            ext = jnp.concatenate([blank, d_pre, blank], axis=0)
            series = series_of(s, h)
            full = None
            for j in range(4):
                moved = ext[3 - j:3 - j + count + 8]
                term = conv_ref[pl.ds(s * 4 + j, 1), lanes] * moved
                full = term if full is None else full + term
                cg[pl.ds((s * 4 + j) * heads + h, 1), :] = jnp.sum(
                    series * moved, axis=0, keepdims=True
                )
            edge_out[h, s * 8:s * 8 + 8, :] = full[:8]
            grads[s][:, lanes] = full[8:].astype(BF16)
            tail[h, s * 8:s * 8 + 8, :] = full[count:]

        @pl.when(z > 0)
        def _():
            edge_copy(h).start()

    early = z < shards // 2
    lag_state = jnp.where(early, 0, SKEW)
    lag_adj = jnp.where(early, SKEW, 0)

    def chain(step, carry):
        hs = step - lag_state
        ha = step - lag_adj

        @pl.when((hs >= 0) & (hs < heads) & (z > 0))
        def _():
            state_copy(hs).wait_recv()

            @pl.when(z < shards - 1)
            def _():
                out_state[hs] = out_state[hs] + advance(n_s[hs], in_state[hs])
                state_copy(hs).start()

        @pl.when((ha >= 0) & (ha < heads) & (z < shards - 1))
        def _():
            adj_copy(ha).wait_recv()

            @pl.when(z > 0)
            def _():
                out_adj[ha] = out_adj[ha] + advance(nt_s[ha], in_adj[ha])
                adj_copy(ha).start()

        @pl.when(step >= SKEW)
        def _():
            finish(step - SKEW)

        return carry

    lax.fori_loop(0, heads + SKEW, chain, 0)

    if scatter:
        piece = cgt.shape[0] // total
        cgt[...] = cg[...].T

        def cg_copy(step):
            peer, where = peer_of(step)
            return pltpu.make_async_remote_copy(
                src_ref=cgt.at[pl.ds(pl.multiple_of(peer * piece, 8), piece), :],
                dst_ref=gathered.at[step],
                send_sem=cg_send.at[step], recv_sem=cg_recv.at[step],
                device_id=where, device_id_type=MESH,
            )

        for step in range(1, total):
            cg_copy(step).start()

    @pl.when(z < shards - 1)
    def _():
        def take(h, carry):
            edge_copy(h).wait_recv()
            return carry

        lax.fori_loop(0, heads, take, 0)

    for h in range(heads):
        for s in range(3):
            lanes = slice(h * width, (h + 1) * width)
            extra = tail[h, s * 8:s * 8 + 8, :] + edge_in[h, s * 8:s * 8 + 8, :]
            grads[s][count - 8:, lanes] = extra.astype(BF16)

    if scatter:
        sums = cgt[pl.ds(pl.multiple_of(mine * piece, 8), piece), :]
        for step in range(1, total):
            cg_copy(step).wait_recv()
            sums = sums + gathered[step]
        conv_out[...] = sums
        for step in range(1, total):
            cg_copy(step).wait_send()
    else:
        conv_out[...] = cg[...]

    @pl.when(z < shards - 1)
    def _():
        for s in range(3):
            halo_copy(s).wait_send()

        def sent(h, carry):
            state_copy(h).wait_send()
            return carry

        lax.fori_loop(0, heads, sent, 0)

    @pl.when(z > 0)
    def _():
        def sent(h, carry):
            adj_copy(h).wait_send()
            edge_copy(h).wait_send()
            return carry

        lax.fori_loop(0, heads, sent, 0)


def per_device(query_raw, key_raw, value_raw, conv_weight, beta_logit, cotangent):
    shards, parts = lax.axis_size("seq"), lax.axis_size("dp")
    heads = beta_logit.shape[1]
    count, channels = query_raw.shape[1:]
    width = channels // heads
    taps = conv_weight.shape[1]
    total = shards * parts
    scatter = total > 1 and width % (8 * total) == 0
    piece = width // total if scatter else 8
    slots = total if scatter else 2
    square = lambda dtype=F32, cols=width: pltpu.VMEM((heads, count, cols), dtype)
    dma = pltpu.SemaphoreType.DMA
    vmem = pl.BlockSpec(memory_space=pltpu.VMEM)
    conv_rows = piece if scatter else width
    outs = pl.pallas_call(
        functools.partial(kernel, shards, parts, scatter),
        out_shape=(
            jax.ShapeDtypeStruct((count, channels), F32),
            jax.ShapeDtypeStruct((count, channels), BF16),
            jax.ShapeDtypeStruct((count, channels), BF16),
            jax.ShapeDtypeStruct((count, channels), BF16),
            jax.ShapeDtypeStruct((heads, count), F32),
            jax.ShapeDtypeStruct((conv_rows, 128), F32),
        ),
        in_specs=[vmem] * 6,
        out_specs=[vmem] * 6,
        scratch_shapes=[
            pltpu.VMEM((3, 16, channels), BF16),
            square(), square(), square(),
            pltpu.VMEM((3, heads, count, width), F32),
            square(), square(), square(), square(F32, 2 * width), square(),
            square(BF16, 2 * width), square(BF16, 2 * width),
            square(), square(), square(), square(),
            pltpu.VMEM((heads, 24, width), F32),
            pltpu.VMEM((heads, 24, width), F32),
            pltpu.VMEM((heads, 24, width), F32),
            pltpu.VMEM((128, width), F32),
            pltpu.VMEM((width, 128), F32),
            pltpu.VMEM((slots, piece, 128), F32),
            dma((3,)), dma((3,)),
            dma((heads,)), dma((heads,)), dma((heads,)), dma((heads,)),
            dma((heads,)), dma((heads,)), dma((slots,)), dma((slots,)),
        ],
        compiler_params=pltpu.CompilerParams(
            collective_id=0, has_side_effects=True, vmem_limit_bytes=48 << 20
        ),
    )(
        query_raw[0], key_raw[0], value_raw[0],
        conv_weight.reshape(3 * taps, channels), beta_logit[0], cotangent[0],
    )
    mixed, d_query, d_key, d_value, d_beta, conv = outs
    used = 3 * taps * heads
    if scatter:
        conv_grad = conv[:, :used].T.reshape(3, taps, heads, piece)
    else:
        conv_grad = lax.psum_scatter(
            conv[:used].reshape(3, taps, heads, width),
            ("seq", "dp"), scatter_dimension=3, tiled=True,
        )
    return (mixed[None], d_query[None], d_key[None], d_value[None], d_beta[None], conv_grad)


def solution(mesh):
    rows = P(("group", "dp"), "seq", "head")
    in_specs = (
        rows, rows, rows,
        P(None, None, "head"),
        P(("group", "dp"), "head", "seq"),
        rows,
    )
    out_specs = (
        rows, rows, rows, rows,
        P(("group", "dp"), "head", "seq"),
        P("group", None, "head", ("seq", "dp")),
    )
    return jax.shard_map(
        per_device, mesh=mesh, in_specs=in_specs, out_specs=out_specs, check_vma=False
    )
```

```python
import functools

import jax
import jax.numpy as jnp
from jax import lax
from jax.experimental import pallas as pl
from jax.experimental.pallas import tpu as pltpu
from jax.sharding import PartitionSpec as P

MESH = pl.DeviceIdType.MESH
F32 = jnp.float32
BF16 = jnp.bfloat16
SKEW = 2
GROUP = 4


def split(x):
    high = x.astype(BF16)
    return high, (x - high.astype(F32)).astype(BF16)


def whole(x):
    return x.astype(BF16), None


def mm(a, b, flip=False):
    ah, al = a
    bh, bl = b
    lhs = ah if al is None else jnp.concatenate([ah, al], axis=1)
    if flip:
        axis_n, axis_k = 0, 1
    else:
        axis_n, axis_k = 1, 0
    n = bh.shape[axis_n]
    rhs = bh if bl is None else jnp.concatenate([bh, bl], axis=axis_n)
    if al is not None:
        rhs = jnp.concatenate([rhs, rhs], axis=axis_k)
    out = lax.dot_general(
        lhs, rhs, (((1,), (axis_k,)), ((), ())), preferred_element_type=F32
    )
    if bl is not None:
        out = out[:, :n] + out[:, n:]
    return out


def kernel(
    shards, parts, scatter,
    q_hbm, k_hbm, v_hbm, conv_hbm, beta_hbm, cot_hbm,
    mixed_ref, dq_ref, dk_ref, dv_ref, dbeta_ref, conv_out,
    q_raw, k_raw, v_raw, conv_ref, beta_ref, cot_ref,
    halo, q_s, k_s, v_s, g_s, p_s, gram_s, inv_s, wu_s, r_s, n_s, nt_s,
    out_state, out_adj, in_state, in_adj, edge_out, edge_in, tail, cg, cgt, gathered,
    halo_send, halo_recv, state_send, state_recv, adj_send, adj_recv,
    edge_send, edge_recv, cg_send, cg_recv, load_sem, beside,
):
    z = lax.axis_index("seq")
    heads = beta_ref.shape[0]
    count, width = q_raw.shape[0], q_raw.shape[1] // heads
    first, last = z == 0, z == shards - 1
    raws = (q_raw, k_raw, v_raw)
    sources = (q_hbm, k_hbm, v_hbm, conv_hbm, beta_hbm, cot_hbm)
    loads = [
        pltpu.make_async_copy(source, kept, load_sem.at[i])
        for i, (source, kept) in enumerate(
            zip(sources, (q_raw, k_raw, v_raw, conv_ref, beta_ref, cot_ref))
        )
    ]
    for load in loads:
        load.start()
    grads = (dq_ref, dk_ref, dv_ref)

    barrier = pltpu.get_barrier_semaphore()
    if scatter:
        total = shards * parts
        column = lax.axis_index("dp")
        mine = z * parts + column

        def peer_of(step):
            peer = lax.rem(mine + step, total)
            return peer, {"seq": peer // parts, "dp": lax.rem(peer, parts)}

        def beside_of(step):
            return {"dp": lax.rem(column + step, parts)}

        for step in range(1, parts):
            pl.semaphore_signal(
                barrier, inc=1, device_id=beside_of(step), device_id_type=MESH
            )

    @pl.when(z > 0)
    def _():
        pl.semaphore_signal(barrier, inc=1, device_id={"seq": z - 1}, device_id_type=MESH)

    @pl.when(z < shards - 1)
    def _():
        pl.semaphore_signal(barrier, inc=1, device_id={"seq": z + 1}, device_id_type=MESH)

    met = parts - 1 if scatter else 0

    @pl.when((z > 0) & (z < shards - 1))
    def _():
        pl.semaphore_wait(barrier, met + 2)

    @pl.when(first | last)
    def _():
        pl.semaphore_wait(barrier, met + 1)

    def halo_copy(s):
        return pltpu.make_async_remote_copy(
            src_ref=sources[s].at[pl.ds(count - 16, 16), :], dst_ref=halo.at[s],
            send_sem=halo_send.at[s], recv_sem=halo_recv.at[s],
            device_id={"seq": z + 1}, device_id_type=MESH,
        )

    def state_copy(h):
        return pltpu.make_async_remote_copy(
            src_ref=out_state.at[h], dst_ref=in_state.at[h],
            send_sem=state_send.at[h], recv_sem=state_recv.at[h],
            device_id={"seq": z + 1}, device_id_type=MESH,
        )

    def adj_copy(h):
        return pltpu.make_async_remote_copy(
            src_ref=out_adj.at[h], dst_ref=in_adj.at[h],
            send_sem=adj_send.at[h], recv_sem=adj_recv.at[h],
            device_id={"seq": z - 1}, device_id_type=MESH,
        )

    def edge_copy(h):
        return pltpu.make_async_remote_copy(
            src_ref=edge_out.at[h], dst_ref=edge_in.at[h],
            send_sem=edge_send.at[h], recv_sem=edge_recv.at[h],
            device_id={"seq": z - 1}, device_id_type=MESH,
        )

    @pl.when(z < shards - 1)
    def _():
        for s in range(3):
            halo_copy(s).start()

    @pl.when(first)
    def _():
        halo[...] = jnp.zeros_like(halo)
        in_state[...] = jnp.zeros_like(in_state)

    @pl.when(last)
    def _():
        in_adj[...] = jnp.zeros_like(in_adj)
        edge_in[...] = jnp.zeros_like(edge_in)

    cg[...] = jnp.zeros_like(cg)
    rows = lax.broadcasted_iota(jnp.int32, (count, count), 0)
    cols = lax.broadcasted_iota(jnp.int32, (count, count), 1)
    apart = rows ^ cols
    strict = rows > cols
    lower = rows >= cols
    eye = rows == cols

    def beta_of(h):
        row = 1.0 / (1.0 + jnp.exp(-beta_ref[pl.ds(h, 1), :]))
        return row, jnp.sum(jnp.where(eye, row, 0.0), axis=1, keepdims=True)

    def lanes_of(h):
        return pl.ds(pl.multiple_of(h * width, width), width)

    def series_of(s, h):
        before = halo[s, :, lanes_of(h)].astype(F32)[8:]
        return jnp.concatenate([before, raws[s][:, lanes_of(h)].astype(F32)], axis=0)

    for load in loads:
        load.wait()

    @pl.when(z > 0)
    def _():
        for s in range(3):
            halo_copy(s).wait_recv()

    def prepare(step, carry):
        ids = [step * GROUP + i for i in range(GROUP)]
        qs, ks, vs = [], [], []
        for h in ids:
            lanes = lanes_of(h)
            made = []
            for s in range(3):
                ext = series_of(s, h)
                pre = conv_ref[s, 0:1, lanes] * ext[5:5 + count]
                for j in range(1, 4):
                    pre = pre + conv_ref[s, j:j + 1, lanes] * ext[5 + j:5 + j + count]
                gate = 1.0 / (1.0 + jnp.exp(-pre))
                act = pre * gate
                slope = gate * (1.0 + pre * (1.0 - gate))
                if s < 2:
                    scale = lax.rsqrt(jnp.sum(act * act, axis=1, keepdims=True) + 1e-06)
                    act = act * scale
                    slope = slope * scale
                g_s[s, h] = slope
                made.append(act)
            q_s[h], k_s[h], v_s[h] = made
            qs.append(made[0])
            ks.append(made[1])
            vs.append(made[2])
        k2 = [split(k) for k in ks]
        gram = [mm(k, k, True) for k in k2]
        score = [jnp.where(lower, mm(split(q), k, True), 0.0) for q, k in zip(qs, k2)]
        betas = [beta_of(h) for h in ids]
        low = [jnp.where(strict, b[1] * g, 0.0) for b, g in zip(betas, gram)]
        inv = [jnp.where(eye, 1.0, 0.0) - jnp.where(apart < 2, a, 0.0) for a in low]
        size = 2
        while size < count:
            band = (apart >= size) & (apart < 2 * size)
            i2 = [split(m) for m in inv]
            part = [mm(split(jnp.where(band, a, 0.0)), m) for a, m in zip(low, i2)]
            inv = [m - mm(n, split(x)) for m, n, x in zip(inv, i2, part)]
            size *= 2
        wu = [
            mm(split(m * b[0]), split(jnp.concatenate([k, v], axis=1)))
            for m, b, k, v in zip(inv, betas, ks, vs)
        ]
        nb = [mm(split(k.T), split(x)) for k, x in zip(ks, wu)]
        reader = [q - mm(split(p), split(x[:, :width])) for q, p, x in zip(qs, score, wu)]
        source = [
            mm(split(r.T), (cot_ref[:, lanes_of(h)], None)) for r, h in zip(reader, ids)
        ]
        for i, h in enumerate(ids):
            out_state[h] = nb[i][:, width:]
            out_adj[h] = source[i]
            p_s[h] = score[i]
            gram_s[h] = gram[i]
            inv_s[h] = inv[i]
            wu_s[h] = wu[i]
            r_s[h] = reader[i]
            n_s[h] = jnp.concatenate(split(nb[i][:, :width]), axis=1)
            nt_s[h] = jnp.concatenate(split(nb[i][:, :width].T), axis=1)

        @pl.when(first)
        def _():
            for h in ids:
                state_copy(h).start()

        @pl.when(last)
        def _():
            for h in ids:
                adj_copy(h).start()

        return carry

    lax.fori_loop(0, heads // GROUP, prepare, 0)

    def advance(pair, value):
        high, low = split(value)
        both = jnp.concatenate([high, low], axis=1)
        out = jnp.dot(pair, jnp.concatenate([both, both], axis=0), preferred_element_type=F32)
        return value - (out[:, :width] + out[:, width:])

    def finish(h):
        lanes = lanes_of(h)
        cot = cot_ref[:, lanes]
        query, key, value = q_s[h], k_s[h], v_s[h]
        score, wu, reader = p_s[h], wu_s[h], r_s[h]
        w_rows, u_rows = wu[:, :width], wu[:, width:]
        state2, adj2 = split(in_state[h]), split(in_adj[h])
        key2 = split(key)
        beta_row, beta_col = beta_of(h)
        reads = mm(split(jnp.concatenate([w_rows, reader], axis=0)), state2)
        corrected = u_rows - reads[:count]
        mixed_ref[:, lanes] = reads[count:] + mm(split(score), split(u_rows))
        d_corr = mm(split(score.T), (cot, None)) + mm(key2, adj2)
        corr2 = split(corrected)
        d_score = jnp.where(lower, mm((cot, None), corr2, True), 0.0)
        back = mm(split(jnp.concatenate([cot.astype(F32), d_corr], axis=0)), state2, True)
        y = mm(split(inv_s[h].T), split(jnp.concatenate([-back[count:], d_corr], axis=1)))
        y_k, y_v = y[:, :width], y[:, width:]
        d_low = jnp.where(strict, -mm(split(y), split(wu), True), 0.0)
        d_beta = jnp.sum(y_k * key + y_v * value + d_low * gram_s[h], axis=1, keepdims=True)
        d_gram = beta_col * d_low
        onto = mm(split(jnp.concatenate([d_score, d_gram + d_gram.T], axis=0)), key2)
        d_query = back[:count] + onto[:count]
        d_key = (
            mm(split(d_score.T), split(query)) + mm(corr2, adj2, True)
            + beta_col * y_k + onto[count:]
        )
        d_value = beta_col * y_v
        d_row = jnp.sum(jnp.where(eye, d_beta, 0.0), axis=0, keepdims=True)
        dbeta_ref[pl.ds(h, 1), :] = d_row * beta_row * (1.0 - beta_row)
        blank = jnp.zeros((8, width), F32)
        for s, grad in enumerate((d_query, d_key, d_value)):
            if s < 2:
                unit = (query, key)[s]
                grad = grad - unit * jnp.sum(grad * unit, axis=1, keepdims=True)
            d_pre = grad * g_s[s, h]
            ext = jnp.concatenate([blank, d_pre, blank], axis=0)
            series = series_of(s, h)
            full = None
            for j in range(4):
                moved = ext[3 - j:3 - j + count + 8]
                term = conv_ref[s, j:j + 1, lanes] * moved
                full = term if full is None else full + term
                cg[pl.ds((s * 4 + j) * heads + h, 1), :] = jnp.sum(
                    series * moved, axis=0, keepdims=True
                )
            edge_out[h, s * 8:s * 8 + 8, :] = full[:8]
            grads[s][:, lanes] = full[8:].astype(BF16)
            tail[h, s * 8:s * 8 + 8, :] = full[count:]

        @pl.when(z > 0)
        def _():
            edge_copy(h).start()

    early = z < shards // 2
    lag_state = jnp.where(early, 0, SKEW)
    lag_adj = jnp.where(early, SKEW, 0)

    def chain(step, carry):
        hs = step - lag_state
        ha = step - lag_adj

        @pl.when((hs >= 0) & (hs < heads) & (z > 0))
        def _():
            state_copy(hs).wait_recv()

            @pl.when(z < shards - 1)
            def _():
                out_state[hs] = out_state[hs] + advance(n_s[hs], in_state[hs])
                state_copy(hs).start()

        @pl.when((ha >= 0) & (ha < heads) & (z < shards - 1))
        def _():
            adj_copy(ha).wait_recv()

            @pl.when(z > 0)
            def _():
                out_adj[ha] = out_adj[ha] + advance(nt_s[ha], in_adj[ha])
                adj_copy(ha).start()

        @pl.when(step >= SKEW)
        def _():
            finish(step - SKEW)

        if scatter:
            @pl.when(step == SKEW)
            def _():
                for other in range(1, parts):
                    pl.semaphore_signal(
                        beside, inc=1, device_id=beside_of(other), device_id_type=MESH
                    )

        return carry

    lax.fori_loop(0, heads + SKEW, chain, 0)

    if scatter:
        if parts > 1:
            pl.semaphore_wait(beside, parts - 1)
        piece = cgt.shape[0] // total
        cgt[...] = cg[...].T

        def cg_copy(step):
            peer, where = peer_of(step)
            return pltpu.make_async_remote_copy(
                src_ref=cgt.at[pl.ds(pl.multiple_of(peer * piece, 8), piece), :],
                dst_ref=gathered.at[step],
                send_sem=cg_send.at[step], recv_sem=cg_recv.at[step],
                device_id=where, device_id_type=MESH,
            )

        for step in range(1, total):
            cg_copy(step).start()

    @pl.when(z < shards - 1)
    def _():
        def take(h, carry):
            edge_copy(h).wait_recv()
            return carry

        lax.fori_loop(0, heads, take, 0)

    for h in range(heads):
        for s in range(3):
            lanes = slice(h * width, (h + 1) * width)
            extra = tail[h, s * 8:s * 8 + 8, :] + edge_in[h, s * 8:s * 8 + 8, :]
            grads[s][count - 8:, lanes] = extra.astype(BF16)

    if scatter:
        sums = cgt[pl.ds(pl.multiple_of(mine * piece, 8), piece), :]
        for step in range(1, total):
            cg_copy(step).wait_recv()
            sums = sums + gathered[step]
        conv_out[...] = sums
        for step in range(1, total):
            cg_copy(step).wait_send()
    else:
        conv_out[...] = cg[...]

    @pl.when(z < shards - 1)
    def _():
        for s in range(3):
            halo_copy(s).wait_send()

        def sent(h, carry):
            state_copy(h).wait_send()
            return carry

        lax.fori_loop(0, heads, sent, 0)

    @pl.when(z > 0)
    def _():
        def sent(h, carry):
            adj_copy(h).wait_send()
            edge_copy(h).wait_send()
            return carry

        lax.fori_loop(0, heads, sent, 0)


def flush(count, *refs):
    blocks, rest = refs[:count], refs[count:]
    if len(rest) == count + 1:
        outs, sems = rest[:count], rest[count]
        extra = ()
    else:
        conv, outs, conv_out, sems, turned = rest[0], rest[1:count + 1], *rest[count + 1:]
        extra = ((turned, conv_out),)
    copies = [
        pltpu.make_async_copy(block, out, sems.at[i])
        for i, (block, out) in enumerate((*zip(blocks, outs), *extra))
    ]
    for copy in copies[:count]:
        copy.start()
    if extra:
        turned[...] = conv[...].T[:turned.shape[0]]
        copies[count].start()
    for copy in copies:
        copy.wait()


def per_device(query_raw, key_raw, value_raw, conv_weight, beta_logit, cotangent):
    shards, parts = lax.axis_size("seq"), lax.axis_size("dp")
    heads = beta_logit.shape[1]
    count, channels = query_raw.shape[1:]
    width = channels // heads
    taps = conv_weight.shape[1]
    total = shards * parts
    scatter = total > 1 and width % (8 * total) == 0
    piece = width // total if scatter else 8
    slots = total if scatter else 2
    square = lambda dtype=F32, cols=width: pltpu.VMEM((heads, count, cols), dtype)
    dma = pltpu.SemaphoreType.DMA
    vmem = pl.BlockSpec(memory_space=pltpu.VMEM)
    conv_rows = piece if scatter else width
    outs = pl.pallas_call(
        functools.partial(kernel, shards, parts, scatter),
        out_shape=(
            jax.ShapeDtypeStruct((count, channels), F32),
            jax.ShapeDtypeStruct((count, channels), BF16),
            jax.ShapeDtypeStruct((count, channels), BF16),
            jax.ShapeDtypeStruct((count, channels), BF16),
            jax.ShapeDtypeStruct((heads, count), F32),
            jax.ShapeDtypeStruct((conv_rows, 128), F32),
        ),
        in_specs=[pl.BlockSpec(memory_space=pltpu.HBM)] * 6,
        out_specs=[vmem] * 6,
        scratch_shapes=[
            pltpu.VMEM((count, channels), BF16),
            pltpu.VMEM((count, channels), BF16),
            pltpu.VMEM((count, channels), BF16),
            pltpu.VMEM((3, taps, channels), F32),
            pltpu.VMEM((heads, count), F32),
            pltpu.VMEM((count, channels), BF16),
            pltpu.VMEM((3, 16, channels), BF16),
            square(), square(), square(),
            pltpu.VMEM((3, heads, count, width), F32),
            square(), square(), square(), square(F32, 2 * width), square(),
            square(BF16, 2 * width), square(BF16, 2 * width),
            square(), square(), square(), square(),
            pltpu.VMEM((heads, 24, width), F32),
            pltpu.VMEM((heads, 24, width), F32),
            pltpu.VMEM((heads, 24, width), F32),
            pltpu.VMEM((128, width), F32),
            pltpu.VMEM((width, 128), F32),
            pltpu.VMEM((slots, piece, 128), F32),
            dma((3,)), dma((3,)),
            dma((heads,)), dma((heads,)), dma((heads,)), dma((heads,)),
            dma((heads,)), dma((heads,)), dma((slots,)), dma((slots,)), dma((6,)),
            pltpu.SemaphoreType.REGULAR,
        ],
        compiler_params=pltpu.CompilerParams(
            collective_id=0, has_side_effects=True, vmem_limit_bytes=48 << 20
        ),
    )(
        *(
            pltpu.with_memory_space_constraint(x, pltpu.HBM)
            for x in (
                query_raw[0], key_raw[0], value_raw[0],
                conv_weight, beta_logit[0], cotangent[0],
            )
        )
    )
    used = 3 * taps * heads
    blocks, conv = outs[:5], outs[5]
    held, free = pl.BlockSpec(memory_space=pl.ANY), pl.BlockSpec(memory_space=pltpu.HBM)
    extra_shape = (jax.ShapeDtypeStruct((used, piece), F32),) if scatter else ()
    flushed = pl.pallas_call(
        functools.partial(flush, 5),
        out_shape=(*(jax.ShapeDtypeStruct(x.shape, x.dtype) for x in blocks), *extra_shape),
        in_specs=[held] * 5 + [vmem] * len(extra_shape),
        out_specs=[free] * (5 + len(extra_shape)),
        scratch_shapes=[
            dma((5 + len(extra_shape),)),
            *(pltpu.VMEM(x.shape, F32) for x in extra_shape),
        ],
        compiler_params=pltpu.CompilerParams(vmem_limit_bytes=2 << 20),
    )(*blocks, *((conv,) if scatter else ()))
    mixed, d_query, d_key, d_value, d_beta = flushed[:5]
    if scatter:
        conv_grad = flushed[5].reshape(3, taps, heads, piece)
    else:
        conv_grad = lax.psum_scatter(
            conv[:used].reshape(3, taps, heads, width),
            ("seq", "dp"), scatter_dimension=3, tiled=True,
        )
    return (mixed[None], d_query[None], d_key[None], d_value[None], d_beta[None], conv_grad)


def solution(mesh):
    rows = P(("group", "dp"), "seq", "head")
    in_specs = (
        rows, rows, rows,
        P(None, None, "head"),
        P(("group", "dp"), "head", "seq"),
        rows,
    )
    out_specs = (
        rows, rows, rows, rows,
        P(("group", "dp"), "head", "seq"),
        P("group", None, "head", ("seq", "dp")),
    )
    return jax.shard_map(
        per_device, mesh=mesh, in_specs=in_specs, out_specs=out_specs, check_vma=False
    )
```

```python
import functools
import itertools

import jax
import jax.numpy as jnp
from jax import lax
from jax.experimental import pallas as pl
from jax.experimental.pallas import tpu as pltpu
from jax.sharding import PartitionSpec as P

MESH = pl.DeviceIdType.MESH
F32 = jnp.float32
BF16 = jnp.bfloat16
SKEW = 3
GROUP = 4
PAIR = 2
REST = 4


def split(x):
    high = x.astype(BF16)
    return high, (x - high.astype(F32)).astype(BF16)


def whole(x):
    return x.astype(BF16), None


def mm(a, b, flip=False):
    ah, al = a
    bh, bl = b
    lhs = ah if al is None else jnp.concatenate([ah, al], axis=1)
    if flip:
        axis_n, axis_k = 0, 1
    else:
        axis_n, axis_k = 1, 0
    n = bh.shape[axis_n]
    rhs = bh if bl is None else jnp.concatenate([bh, bl], axis=axis_n)
    if al is not None:
        rhs = jnp.concatenate([rhs, rhs], axis=axis_k)
    out = lax.dot_general(
        lhs, rhs, (((1,), (axis_k,)), ((), ())), preferred_element_type=F32
    )
    if bl is not None:
        out = out[:, :n] + out[:, n:]
    return out


def kernel(
    shards, parts, scatter,
    q_hbm, k_hbm, v_hbm, conv_hbm, beta_hbm, cot_hbm,
    mixed_ref, dq_ref, dk_ref, dv_ref, dbeta_ref, conv_out,
    q_raw, k_raw, v_raw, conv_ref, beta_ref, cot_ref,
    halo, q_s, k_s, v_s, g_s, p_s, gram_s, inv_s, wu_s, r_s, n_s, nt_s,
    out_state, out_adj, in_state, in_adj, edge_out, edge_in, tail, cg, cgt, gathered,
    halo_send, halo_recv, state_send, state_recv, adj_send, adj_recv,
    edge_send, edge_recv, cg_send, cg_recv, load_sem, beside,
):
    z = lax.axis_index("seq")
    heads = beta_ref.shape[0]
    count, width = q_raw.shape[0], q_raw.shape[1] // heads
    first, last = z == 0, z == shards - 1
    raws = (q_raw, k_raw, v_raw)
    sources = (q_hbm, k_hbm, v_hbm, conv_hbm, beta_hbm, cot_hbm)
    loads = [
        pltpu.make_async_copy(source, kept, load_sem.at[i])
        for i, (source, kept) in enumerate(
            zip(sources, (q_raw, k_raw, v_raw, conv_ref, beta_ref, cot_ref))
        )
    ]
    for load in loads:
        load.start()
    grads = (dq_ref, dk_ref, dv_ref)

    barrier = pltpu.get_barrier_semaphore()
    if scatter:
        total = shards * parts
        column = lax.axis_index("dp")
        mine = z * parts + column

        def peer_of(step):
            peer = lax.rem(mine + step, total)
            return peer, {"seq": peer // parts, "dp": lax.rem(peer, parts)}

        def beside_of(step):
            return {"dp": lax.rem(column + step, parts)}

        for step in range(1, parts):
            pl.semaphore_signal(
                barrier, inc=1, device_id=beside_of(step), device_id_type=MESH
            )

    @pl.when(z > 0)
    def _():
        pl.semaphore_signal(barrier, inc=1, device_id={"seq": z - 1}, device_id_type=MESH)

    @pl.when(z < shards - 1)
    def _():
        pl.semaphore_signal(barrier, inc=1, device_id={"seq": z + 1}, device_id_type=MESH)

    met = parts - 1 if scatter else 0

    @pl.when((z > 0) & (z < shards - 1))
    def _():
        pl.semaphore_wait(barrier, met + 2)

    @pl.when(first | last)
    def _():
        pl.semaphore_wait(barrier, met + 1)

    def halo_copy(s):
        return pltpu.make_async_remote_copy(
            src_ref=sources[s].at[pl.ds(count - 16, 16), :], dst_ref=halo.at[s],
            send_sem=halo_send.at[s], recv_sem=halo_recv.at[s],
            device_id={"seq": z + 1}, device_id_type=MESH,
        )

    def state_copy(h):
        return pltpu.make_async_remote_copy(
            src_ref=out_state.at[h], dst_ref=in_state.at[h],
            send_sem=state_send.at[h], recv_sem=state_recv.at[h],
            device_id={"seq": z + 1}, device_id_type=MESH,
        )

    def adj_copy(h):
        return pltpu.make_async_remote_copy(
            src_ref=out_adj.at[h], dst_ref=in_adj.at[h],
            send_sem=adj_send.at[h], recv_sem=adj_recv.at[h],
            device_id={"seq": z - 1}, device_id_type=MESH,
        )

    def edge_copy(h):
        return pltpu.make_async_remote_copy(
            src_ref=edge_out.at[h], dst_ref=edge_in.at[h],
            send_sem=edge_send.at[h], recv_sem=edge_recv.at[h],
            device_id={"seq": z - 1}, device_id_type=MESH,
        )

    @pl.when(z < shards - 1)
    def _():
        for s in range(3):
            halo_copy(s).start()

    @pl.when(first)
    def _():
        halo[...] = jnp.zeros_like(halo)
        in_state[...] = jnp.zeros_like(in_state)

    @pl.when(last)
    def _():
        in_adj[...] = jnp.zeros_like(in_adj)
        edge_in[...] = jnp.zeros_like(edge_in)

    cg[...] = jnp.zeros_like(cg)
    rows = lax.broadcasted_iota(jnp.int32, (count, count), 0)
    cols = lax.broadcasted_iota(jnp.int32, (count, count), 1)
    apart = rows ^ cols
    strict = rows > cols
    lower = rows >= cols
    eye = rows == cols

    def beta_of(h):
        row = 1.0 / (1.0 + jnp.exp(-beta_ref[pl.ds(h, 1), :]))
        return row, jnp.sum(jnp.where(eye, row, 0.0), axis=1, keepdims=True)

    def lanes_of(h):
        return pl.ds(pl.multiple_of(h * width, width), width)

    def series_of(s, h):
        before = halo[s, :, lanes_of(h)].astype(F32)[8:]
        return jnp.concatenate([before, raws[s][:, lanes_of(h)].astype(F32)], axis=0)

    for load in loads:
        load.wait()

    @pl.when(z > 0)
    def _():
        for s in range(3):
            halo_copy(s).wait_recv()

    def prepare(step, carry):
        ids = [step * GROUP + i for i in range(GROUP)]
        qs, ks, vs = [], [], []
        for h in ids:
            lanes = lanes_of(h)
            made = []
            for s in range(3):
                ext = series_of(s, h)
                pre = conv_ref[s, 0:1, lanes] * ext[5:5 + count]
                for j in range(1, 4):
                    pre = pre + conv_ref[s, j:j + 1, lanes] * ext[5 + j:5 + j + count]
                gate = 1.0 / (1.0 + jnp.exp(-pre))
                act = pre * gate
                slope = gate * (1.0 + pre * (1.0 - gate))
                if s < 2:
                    scale = lax.rsqrt(jnp.sum(act * act, axis=1, keepdims=True) + 1e-06)
                    act = act * scale
                    slope = slope * scale
                g_s[s, h] = slope
                made.append(act)
            q_s[h], k_s[h], v_s[h] = made
            qs.append(made[0])
            ks.append(made[1])
            vs.append(made[2])
        k2 = [split(k) for k in ks]
        gram = [mm(k, k, True) for k in k2]
        score = [jnp.where(lower, mm(split(q), k, True), 0.0) for q, k in zip(qs, k2)]
        betas = [beta_of(h) for h in ids]
        low = [jnp.where(strict, b[1] * g, 0.0) for b, g in zip(betas, gram)]
        inv = [jnp.where(eye, 1.0, 0.0) - jnp.where(apart < 2, a, 0.0) for a in low]
        size = 2
        while size < count:
            band = (apart >= size) & (apart < 2 * size)
            i2 = [split(m) for m in inv]
            part = [mm(split(jnp.where(band, a, 0.0)), m) for a, m in zip(low, i2)]
            inv = [m - mm(n, split(x)) for m, n, x in zip(inv, i2, part)]
            size *= 2
        wu = [
            mm(split(m * b[0]), split(jnp.concatenate([k, v], axis=1)))
            for m, b, k, v in zip(inv, betas, ks, vs)
        ]
        nb = [mm(split(k.T), split(x)) for k, x in zip(ks, wu)]
        reader = [q - mm(split(p), split(x[:, :width])) for q, p, x in zip(qs, score, wu)]
        source = [
            mm(split(r.T), (cot_ref[:, lanes_of(h)], None)) for r, h in zip(reader, ids)
        ]
        for i, h in enumerate(ids):
            out_state[h] = nb[i][:, width:]
            out_adj[h] = source[i]
            p_s[h] = score[i]
            gram_s[h] = gram[i]
            inv_s[h] = inv[i]
            wu_s[h] = wu[i]
            r_s[h] = reader[i]
            n_s[h] = jnp.concatenate(split(nb[i][:, :width]), axis=1)
            nt_s[h] = jnp.concatenate(split(nb[i][:, :width].T), axis=1)

        @pl.when(first)
        def _():
            for h in ids:
                state_copy(h).start()

        @pl.when(last)
        def _():
            for h in ids:
                adj_copy(h).start()

        return carry

    lax.fori_loop(0, heads // GROUP, prepare, 0)

    def advance(pair, value):
        high, low = split(value)
        both = jnp.concatenate([high, low], axis=1)
        out = jnp.dot(pair, jnp.concatenate([both, both], axis=0), preferred_element_type=F32)
        return value - (out[:, :width] + out[:, width:])

    def finish(h):
        lanes = lanes_of(h)
        cot = cot_ref[:, lanes]
        query, key, value = q_s[h], k_s[h], v_s[h]
        score, wu, reader = p_s[h], wu_s[h], r_s[h]
        w_rows, u_rows = wu[:, :width], wu[:, width:]
        state2, adj2 = split(in_state[h]), split(in_adj[h])
        key2 = split(key)
        beta_row, beta_col = beta_of(h)
        reads = mm(split(jnp.concatenate([w_rows, reader], axis=0)), state2)
        yield
        corrected = u_rows - reads[:count]
        mixed_ref[:, lanes] = reads[count:] + mm(split(score), split(u_rows))
        d_corr = mm(split(score.T), (cot, None)) + mm(key2, adj2)
        yield
        corr2 = split(corrected)
        d_score = jnp.where(lower, mm((cot, None), corr2, True), 0.0)
        yield
        back = mm(split(jnp.concatenate([cot.astype(F32), d_corr], axis=0)), state2, True)
        yield
        y = mm(split(inv_s[h].T), split(jnp.concatenate([-back[count:], d_corr], axis=1)))
        y_k, y_v = y[:, :width], y[:, width:]
        yield
        d_low = jnp.where(strict, -mm(split(y), split(wu), True), 0.0)
        yield
        d_beta = jnp.sum(y_k * key + y_v * value + d_low * gram_s[h], axis=1, keepdims=True)
        d_gram = beta_col * d_low
        onto = mm(split(jnp.concatenate([d_score, d_gram + d_gram.T], axis=0)), key2)
        yield
        d_query = back[:count] + onto[:count]
        d_key = (
            mm(split(d_score.T), split(query)) + mm(corr2, adj2, True)
            + beta_col * y_k + onto[count:]
        )
        yield
        d_value = beta_col * y_v
        d_row = jnp.sum(jnp.where(eye, d_beta, 0.0), axis=0, keepdims=True)
        dbeta_ref[pl.ds(h, 1), :] = d_row * beta_row * (1.0 - beta_row)
        blank = jnp.zeros((8, width), F32)
        for s, grad in enumerate((d_query, d_key, d_value)):
            if s < 2:
                unit = (query, key)[s]
                grad = grad - unit * jnp.sum(grad * unit, axis=1, keepdims=True)
            d_pre = grad * g_s[s, h]
            ext = jnp.concatenate([blank, d_pre, blank], axis=0)
            yield
            series = series_of(s, h)
            full = None
            for j in range(4):
                moved = ext[3 - j:3 - j + count + 8]
                term = conv_ref[s, j:j + 1, lanes] * moved
                full = term if full is None else full + term
                cg[pl.ds((s * 4 + j) * heads + h, 1), :] = jnp.sum(
                    series * moved, axis=0, keepdims=True
                )
            edge_out[h, s * 8:s * 8 + 8, :] = full[:8]
            grads[s][:, lanes] = full[8:].astype(BF16)
            tail[h, s * 8:s * 8 + 8, :] = full[count:]

    early = z < shards // 2
    lag_state = jnp.where(early, 0, SKEW)
    lag_end = jnp.where(first | last, SKEW, SKEW + REST)
    lag_adj = jnp.where(early, SKEW, 0)

    def chain(step, carry):
        hs = step - lag_state
        ha = step - lag_adj

        @pl.when((hs >= 0) & (hs < heads) & (z > 0))
        def _():
            state_copy(hs).wait_recv()

            @pl.when(z < shards - 1)
            def _():
                out_state[hs] = out_state[hs] + advance(n_s[hs], in_state[hs])
                state_copy(hs).start()

        @pl.when((ha >= 0) & (ha < heads) & (z < shards - 1))
        def _():
            adj_copy(ha).wait_recv()

            @pl.when(z > 0)
            def _():
                out_adj[ha] = out_adj[ha] + advance(nt_s[ha], in_adj[ha])
                adj_copy(ha).start()

        done = step - lag_end

        @pl.when((done >= 0) & (done < heads) & (lax.rem(done, PAIR) == PAIR - 1))
        def _():
            ids = [done - PAIR + 1 + i for i in range(PAIR)]
            for _ in itertools.zip_longest(*[finish(h) for h in ids]):
                pass

            @pl.when(z > 0)
            def _():
                for h in ids:
                    edge_copy(h).start()

        if scatter:
            @pl.when(step == SKEW)
            def _():
                for other in range(1, parts):
                    pl.semaphore_signal(
                        beside, inc=1, device_id=beside_of(other), device_id_type=MESH
                    )

        return carry

    lax.fori_loop(0, heads + SKEW + REST, chain, 0)

    if scatter:
        if parts > 1:
            pl.semaphore_wait(beside, parts - 1)
        piece = cgt.shape[0] // total
        cgt[...] = cg[...].T

        def cg_copy(step):
            peer, where = peer_of(step)
            return pltpu.make_async_remote_copy(
                src_ref=cgt.at[pl.ds(pl.multiple_of(peer * piece, 8), piece), :],
                dst_ref=gathered.at[step],
                send_sem=cg_send.at[step], recv_sem=cg_recv.at[step],
                device_id=where, device_id_type=MESH,
            )

        for step in range(1, total):
            cg_copy(step).start()

    @pl.when(z < shards - 1)
    def _():
        def take(h, carry):
            edge_copy(h).wait_recv()
            return carry

        lax.fori_loop(0, heads, take, 0)

    for h in range(heads):
        for s in range(3):
            lanes = slice(h * width, (h + 1) * width)
            extra = tail[h, s * 8:s * 8 + 8, :] + edge_in[h, s * 8:s * 8 + 8, :]
            grads[s][count - 8:, lanes] = extra.astype(BF16)

    if scatter:
        sums = cgt[pl.ds(pl.multiple_of(mine * piece, 8), piece), :]
        for step in range(1, total):
            cg_copy(step).wait_recv()
            sums = sums + gathered[step]
        conv_out[...] = sums
        for step in range(1, total):
            cg_copy(step).wait_send()
    else:
        conv_out[...] = cg[...]

    @pl.when(z < shards - 1)
    def _():
        for s in range(3):
            halo_copy(s).wait_send()

        def sent(h, carry):
            state_copy(h).wait_send()
            return carry

        lax.fori_loop(0, heads, sent, 0)

    @pl.when(z > 0)
    def _():
        def sent(h, carry):
            adj_copy(h).wait_send()
            edge_copy(h).wait_send()
            return carry

        lax.fori_loop(0, heads, sent, 0)


def flush(count, *refs):
    blocks, rest = refs[:count], refs[count:]
    if len(rest) == count + 1:
        outs, sems = rest[:count], rest[count]
        extra = ()
    else:
        conv, outs, conv_out, sems, turned = rest[0], rest[1:count + 1], *rest[count + 1:]
        extra = ((turned, conv_out),)
    copies = [
        pltpu.make_async_copy(block, out, sems.at[i])
        for i, (block, out) in enumerate((*zip(blocks, outs), *extra))
    ]
    for copy in copies[:count]:
        copy.start()
    if extra:
        turned[...] = conv[...].T[:turned.shape[0]]
        copies[count].start()
    for copy in copies:
        copy.wait()


def per_device(query_raw, key_raw, value_raw, conv_weight, beta_logit, cotangent):
    shards, parts = lax.axis_size("seq"), lax.axis_size("dp")
    heads = beta_logit.shape[1]
    count, channels = query_raw.shape[1:]
    width = channels // heads
    taps = conv_weight.shape[1]
    total = shards * parts
    scatter = total > 1 and width % (8 * total) == 0
    piece = width // total if scatter else 8
    slots = total if scatter else 2
    square = lambda dtype=F32, cols=width: pltpu.VMEM((heads, count, cols), dtype)
    dma = pltpu.SemaphoreType.DMA
    vmem = pl.BlockSpec(memory_space=pltpu.VMEM)
    conv_rows = piece if scatter else width
    outs = pl.pallas_call(
        functools.partial(kernel, shards, parts, scatter),
        out_shape=(
            jax.ShapeDtypeStruct((count, channels), F32),
            jax.ShapeDtypeStruct((count, channels), BF16),
            jax.ShapeDtypeStruct((count, channels), BF16),
            jax.ShapeDtypeStruct((count, channels), BF16),
            jax.ShapeDtypeStruct((heads, count), F32),
            jax.ShapeDtypeStruct((conv_rows, 128), F32),
        ),
        in_specs=[pl.BlockSpec(memory_space=pltpu.HBM)] * 6,
        out_specs=[vmem] * 6,
        scratch_shapes=[
            pltpu.VMEM((count, channels), BF16),
            pltpu.VMEM((count, channels), BF16),
            pltpu.VMEM((count, channels), BF16),
            pltpu.VMEM((3, taps, channels), F32),
            pltpu.VMEM((heads, count), F32),
            pltpu.VMEM((count, channels), BF16),
            pltpu.VMEM((3, 16, channels), BF16),
            square(), square(), square(),
            pltpu.VMEM((3, heads, count, width), F32),
            square(), square(), square(), square(F32, 2 * width), square(),
            square(BF16, 2 * width), square(BF16, 2 * width),
            square(), square(), square(), square(),
            pltpu.VMEM((heads, 24, width), F32),
            pltpu.VMEM((heads, 24, width), F32),
            pltpu.VMEM((heads, 24, width), F32),
            pltpu.VMEM((128, width), F32),
            pltpu.VMEM((width, 128), F32),
            pltpu.VMEM((slots, piece, 128), F32),
            dma((3,)), dma((3,)),
            dma((heads,)), dma((heads,)), dma((heads,)), dma((heads,)),
            dma((heads,)), dma((heads,)), dma((slots,)), dma((slots,)), dma((6,)),
            pltpu.SemaphoreType.REGULAR,
        ],
        compiler_params=pltpu.CompilerParams(
            collective_id=0, has_side_effects=True, vmem_limit_bytes=48 << 20
        ),
    )(
        *(
            pltpu.with_memory_space_constraint(x, pltpu.HBM)
            for x in (
                query_raw[0], key_raw[0], value_raw[0],
                conv_weight, beta_logit[0], cotangent[0],
            )
        )
    )
    used = 3 * taps * heads
    blocks, conv = outs[:5], outs[5]
    held, free = pl.BlockSpec(memory_space=pl.ANY), pl.BlockSpec(memory_space=pltpu.HBM)
    extra_shape = (jax.ShapeDtypeStruct((used, piece), F32),) if scatter else ()
    flushed = pl.pallas_call(
        functools.partial(flush, 5),
        out_shape=(*(jax.ShapeDtypeStruct(x.shape, x.dtype) for x in blocks), *extra_shape),
        in_specs=[held] * 5 + [vmem] * len(extra_shape),
        out_specs=[free] * (5 + len(extra_shape)),
        scratch_shapes=[
            dma((5 + len(extra_shape),)),
            *(pltpu.VMEM(x.shape, F32) for x in extra_shape),
        ],
        compiler_params=pltpu.CompilerParams(vmem_limit_bytes=2 << 20),
    )(*blocks, *((conv,) if scatter else ()))
    mixed, d_query, d_key, d_value, d_beta = flushed[:5]
    if scatter:
        conv_grad = flushed[5].reshape(3, taps, heads, piece)
    else:
        conv_grad = lax.psum_scatter(
            conv[:used].reshape(3, taps, heads, width),
            ("seq", "dp"), scatter_dimension=3, tiled=True,
        )
    return (mixed[None], d_query[None], d_key[None], d_value[None], d_beta[None], conv_grad)


def solution(mesh):
    rows = P(("group", "dp"), "seq", "head")
    in_specs = (
        rows, rows, rows,
        P(None, None, "head"),
        P(("group", "dp"), "head", "seq"),
        rows,
    )
    out_specs = (
        rows, rows, rows, rows,
        P(("group", "dp"), "head", "seq"),
        P("group", None, "head", ("seq", "dp")),
    )
    return jax.shard_map(
        per_device, mesh=mesh, in_specs=in_specs, out_specs=out_specs, check_vma=False
    )
```
